256 devices in a mesh: tok: 8 (over x, core), hid: 32 (over y, z).
Axes of the slice: x: 4, y: 4, z: 8, core: 2. Of those that a mesh axis runs over, the one named last changes fastest.
Arguments:
- layer_input: bfloat16 [6144, 5120], P(('tok', 'hid')), may hold values from -6 to 6
- output_grad: bfloat16 [6144, 5120], P(('tok', 'hid')), may hold values from -6 to 6
- gate_weight: bfloat16 [5120, 8192], P(None, 'hid'), may hold values from -0.078125 to 0.078125
- up_weight: bfloat16 [5120, 8192], P(None, 'hid'), may hold values from -0.078125 to 0.078125
- down_weight: bfloat16 [8192, 5120], P('hid'), may hold values from -0.0625 to 0.0625
- block_lists: int32 [48, 32], P('tok'), may hold values from 0 to 63, as said below
- block_count: int32 [48], P('tok'), may hold values from 8 to 32, as said below
Outputs:
- input_grad: bfloat16 [6144, 5120], P(('tok', 'hid'))
- gate_grad: bfloat16 [5120, 8192], P('tok', 'hid')
- up_grad: bfloat16 [5120, 8192], P('tok', 'hid')
- down_grad: bfloat16 [8192, 5120], P('hid', 'tok')
The draws below stay inside these ranges and needn't reach their ends.
Inputs may be any that keep to these rules, and one draw needn't show every extreme that they name: Each row of block_lists holds 32 different block numbers; entries past the tile's count are valid block numbers too and are not active. `block_count`: some tile uses all 32 slots and some tile uses 8.
All inputs are finite; a program needn't handle non-finite values.
Results may differ from the reference program's by a relative error of at most 0.015.
Values may be sent and summed in bfloat16 or wider, within the bound.
No kernel may reach another device: no remote copies, remote signals or barrier semaphores. Data moves between devices by JAX's collectives and lax.ppermute only.
A program may use at most 128 MiB of HBM per device.

```python
import math
import jax
import jax.numpy as jnp
from jax import lax

D = 5120
FF = 8192
BLOCK = 128
TILE = 128
KMAX = 32
TOKENS = 6144
NTILES = 48
N_HID = 32


def make_lists(key):
    base_key = jax.random.fold_in(key, 31)
    key_favour, key_noise, key_count, key_full, key_short = jax.random.split(base_key, 5)
    overall_block_count = FF // BLOCK
    preference_weight = jax.random.randint(key_favour, (overall_block_count,), 0, 3) * (overall_block_count * 4)
    random_jitter = jax.random.randint(key_noise, (NTILES, overall_block_count), 0, overall_block_count * 8)
    complete_tile = jax.random.randint(key_full, (), 0, NTILES)
    short_tile = (complete_tile + 1 + jax.random.randint(key_short, (), 0, NTILES - 1)) % NTILES
    rows_per_tile = jnp.arange(NTILES)
    block_column_span = jnp.arange(overall_block_count)
    tile_stops = (block_column_span == 0) | (block_column_span == overall_block_count - 1)
    score_boost = jnp.where((rows_per_tile[:, None] == complete_tile) & tile_stops[None, :], overall_block_count * 32, 0)
    predictor_scores = (random_jitter + preference_weight[None, :] + score_boost) * overall_block_count + block_column_span[None, :]
    top_scores, block_ids = jax.lax.top_k(predictor_scores, KMAX)
    counts = jax.random.randint(key_count, (NTILES,), KMAX // 4, KMAX + 1)
    counts = jnp.where(rows_per_tile == complete_tile, KMAX, counts)
    counts = jnp.where(rows_per_tile == short_tile, KMAX // 4, counts)
    return (block_ids.astype(jnp.int32), counts.astype(jnp.int32))


def draw_block_lists(key, part):
    return make_lists(key)[0]


def draw_block_count(key, part):
    return make_lists(key)[1]


def shard_levels(key, shape, pieces, least, largest):
    level = 1.0
    for axis_at, shards_of in pieces:
        steps = jax.random.uniform(jax.random.fold_in(jax.random.fold_in(key, 6), axis_at), (shards_of,), jnp.float32, least / len(pieces), largest / len(pieces))
        level = level * jnp.repeat(jnp.exp(steps), shape[axis_at] // shards_of).reshape((-1,) + (1,) * (len(shape) - 1 - axis_at))
    return level


def scatter_about(stream_key, extent, width, reach, cuts=(), dtype=jnp.bfloat16):
    loudness = shard_levels(stream_key, extent, cuts, -0.22, 0.18) if cuts else 1.0
    array = jax.random.normal(stream_key, extent, jnp.float32) * width * loudness
    return jnp.minimum(jnp.maximum(array, -reach), reach).astype(dtype)


def setup_inputs(seed: int = 0) -> dict:
    seeds = jax.random.split(jax.random.key(seed), 8)
    return {
        "layer_input": scatter_about(seeds[0], (TOKENS, D), 1.0, 6.0, ((0, 256),)),
        "output_grad": scatter_about(seeds[1], (TOKENS, D), 1.0, 6.0, ((0, 256),)),
        "gate_weight": scatter_about(seeds[2], (D, FF), D ** -0.5, 0.078125, ((1, 32),)),
        "up_weight": scatter_about(seeds[3], (D, FF), D ** -0.5, 0.078125, ((1, 32),)),
        "down_weight": scatter_about(seeds[4], (FF, D), FF ** -0.5, 0.0625, ((0, 32),)),
        "block_lists": draw_block_lists(jax.random.fold_in(seeds[7], 71), 0),
        "block_count": draw_block_count(jax.random.fold_in(seeds[7], 71), 0),
    }


def reference(layer_input, output_grad, gate_weight, up_weight, down_weight, block_lists, block_count):
    overall_block_count = FF // BLOCK
    in_list = jnp.arange(KMAX)[None, :] < block_count[:, None]
    hits = (block_lists[:, :, None] == jnp.arange(overall_block_count)[None, None, :]) & in_list[:, :, None]
    tile_mask = jnp.any(hits, axis=1).astype(jnp.float32)
    unit_mask = jnp.repeat(jnp.repeat(tile_mask, TILE, axis=0), BLOCK, axis=1)
    contract_last = (((1,), (1,)), ((), ()))
    contract_first = (((0,), (0,)), ((), ()))
    gate_pre = jnp.dot(layer_input, gate_weight, preferred_element_type=jnp.float32)
    up_pre = jnp.dot(layer_input, up_weight, preferred_element_type=jnp.float32)
    grad_hidden = lax.dot_general(output_grad, down_weight, contract_last, preferred_element_type=jnp.float32)
    sigmoid_g = jax.nn.sigmoid(gate_pre)
    silu_g = gate_pre * sigmoid_g
    hidden = (unit_mask * silu_g * up_pre).astype(jnp.bfloat16)
    grad_gate = (unit_mask * grad_hidden * up_pre * sigmoid_g * (1.0 + gate_pre * (1.0 - sigmoid_g))).astype(jnp.bfloat16)
    grad_up = (unit_mask * grad_hidden * silu_g).astype(jnp.bfloat16)
    group_width = FF // N_HID

    def add_group(shard, total):
        start = (shard * group_width).astype(jnp.int32)
        part_gate = lax.dynamic_slice_in_dim(grad_gate, start, group_width, 1)
        part_up = lax.dynamic_slice_in_dim(grad_up, start, group_width, 1)
        weight_gate = lax.dynamic_slice_in_dim(gate_weight, start, group_width, 1)
        weight_up = lax.dynamic_slice_in_dim(up_weight, start, group_width, 1)
        partial_value = lax.dot_general(part_gate, weight_gate, contract_last, preferred_element_type=jnp.float32)
        partial_value = partial_value + lax.dot_general(part_up, weight_up, contract_last, preferred_element_type=jnp.float32)
        rounded = lax.optimization_barrier(partial_value.astype(jnp.bfloat16))
        return total + rounded.astype(jnp.float32)
    summed = lax.fori_loop(0, N_HID, add_group, jnp.zeros((TOKENS, D), jnp.float32))
    input_grad = summed.astype(jnp.bfloat16)
    scale = 1.0 / math.sqrt(TOKENS)
    gate_grad = (lax.dot_general(layer_input, grad_gate, contract_first, preferred_element_type=jnp.float32) * scale).astype(jnp.bfloat16)
    up_grad = (lax.dot_general(layer_input, grad_up, contract_first, preferred_element_type=jnp.float32) * scale).astype(jnp.bfloat16)
    down_grad = (lax.dot_general(hidden, output_grad, contract_first, preferred_element_type=jnp.float32) * scale).astype(jnp.bfloat16)
    return (input_grad, gate_grad, up_grad, down_grad)
```

```python
import math

import jax
import jax.numpy as jnp
from jax import lax
from jax.sharding import Mesh, PartitionSpec as P

BLOCK = 128
TILE = 128


def to_tiles(a):
    r, c = a.shape
    return a.reshape(r // 8, 8, c // 128, 128).transpose(0, 2, 1, 3).reshape(r * c // 128, 128)


def from_tiles(a, r, c):
    return a.reshape(r // 8, c // 128, 8, 128).transpose(0, 2, 1, 3).reshape(r, c)


def tile_activity(block_lists, block_count, local_blocks):
    in_list = jnp.arange(block_lists.shape[1])[None, :] < block_count[:, None]
    hits = (block_lists[:, :, None] == local_blocks[None, None, :]) & in_list[:, :, None]
    return jnp.any(hits, axis=1)


def unit_grads(gate_pre, up_pre, grad_hidden, unit_mask):
    sigmoid_g = jax.nn.sigmoid(gate_pre)
    silu_g = gate_pre * sigmoid_g
    hidden = (unit_mask * silu_g * up_pre).astype(jnp.bfloat16)
    grad_gate = (
        unit_mask * grad_hidden * up_pre * sigmoid_g * (1.0 + gate_pre * (1.0 - sigmoid_g))
    ).astype(jnp.bfloat16)
    grad_up = (unit_mask * grad_hidden * silu_g).astype(jnp.bfloat16)
    return (hidden, grad_gate, grad_up)


def body(layer_input, output_grad, gate_weight, up_weight, down_weight, block_lists, block_count):
    contract_last = (((1,), (1,)), ((), ()))
    contract_first = (((0,), (0,)), ((), ()))
    rows, d_model = layer_input.shape
    width = gate_weight.shape[1]
    blocks_here = width // BLOCK
    local_blocks = lax.axis_index("hid") * blocks_here + jnp.arange(blocks_here, dtype=jnp.int32)
    active = tile_activity(block_lists, block_count, local_blocks)
    tok_rows = rows * lax.axis_size("hid")
    inputs_full = from_tiles(lax.all_gather(to_tiles(layer_input), "hid", axis=0, tiled=True), tok_rows, d_model)
    grads_full = from_tiles(lax.all_gather(to_tiles(output_grad), "hid", axis=0, tiled=True), tok_rows, d_model)
    tiles_here = tok_rows // TILE
    unit_mask = jnp.broadcast_to(
        active.astype(jnp.float32)[:, None, :, None], (tiles_here, TILE, blocks_here, BLOCK)
    ).reshape(tok_rows, width)
    gate_pre = jnp.dot(inputs_full, gate_weight, preferred_element_type=jnp.float32)
    up_pre = jnp.dot(inputs_full, up_weight, preferred_element_type=jnp.float32)
    grad_hidden = lax.dot_general(
        grads_full, down_weight, contract_last, preferred_element_type=jnp.float32
    )
    hidden, grad_gate, grad_up = unit_grads(gate_pre, up_pre, grad_hidden, unit_mask)
    total = lax.dot_general(
        grad_gate, gate_weight, contract_last, preferred_element_type=jnp.float32
    )
    partial = (
        total
        + lax.dot_general(grad_up, up_weight, contract_last, preferred_element_type=jnp.float32)
    ).astype(jnp.bfloat16)
    input_grad = from_tiles(
        lax.psum_scatter(to_tiles(partial), "hid", scatter_dimension=0, tiled=True), rows, d_model
    )
    scale = 1.0 / math.sqrt(tok_rows * lax.axis_size("tok"))
    term_gate = lax.dot_general(
        inputs_full, grad_gate, contract_first, preferred_element_type=jnp.float32
    )
    term_up = lax.dot_general(
        inputs_full, grad_up, contract_first, preferred_element_type=jnp.float32
    )
    term_down = lax.dot_general(
        grads_full, hidden, contract_first, preferred_element_type=jnp.float32
    )
    stacked = lax.psum_scatter(
        (jnp.concatenate([term_gate, term_up, term_down], axis=1) * scale).astype(jnp.bfloat16),
        "tok",
        scatter_dimension=0,
        tiled=True,
    ).astype(jnp.float32)
    gate_grad = stacked[:, :width].astype(jnp.bfloat16)
    up_grad = stacked[:, width : 2 * width].astype(jnp.bfloat16)
    down_grad = stacked[:, 2 * width :].T.astype(jnp.bfloat16)
    return (input_grad, gate_grad, up_grad, down_grad)


def solution(mesh):
    in_specs = (
        P(("tok", "hid"), None),
        P(("tok", "hid"), None),
        P(None, "hid"),
        P(None, "hid"),
        P("hid", None),
        P("tok", None),
        P("tok"),
    )
    out_specs = (P(("tok", "hid"), None), P("tok", "hid"), P("tok", "hid"), P("hid", "tok"))
    return jax.shard_map(body, mesh=mesh, in_specs=in_specs, out_specs=out_specs, check_vma=False)
```

```python
import math

import jax
import jax.numpy as jnp
from jax import lax
from jax.experimental import pallas as pl
from jax.experimental.pallas import tpu as pltpu
from jax.sharding import PartitionSpec as P

BLOCK = 128
TILE = 128
NX, NC, NY, NZ = 4, 2, 4, 8
LAST = (((1,), (1,)), ((), ()))
F32 = jnp.float32
BF16 = jnp.bfloat16


def shift(value, dim, step):
    if dim == "x":
        axis = "tok"
        perm = [(x * NC + c, (x + step) % NX * NC + c) for x in range(NX) for c in range(NC)]
    elif dim == "c":
        axis = "tok"
        perm = [(x * NC + c, x * NC + (c + step) % NC) for x in range(NX) for c in range(NC)]
    elif dim == "y":
        axis = "hid"
        perm = [(y * NZ + z, (y + step) % NY * NZ + z) for y in range(NY) for z in range(NZ)]
    else:
        axis = "hid"
        perm = [(y * NZ + z, y * NZ + (z + step) % NZ) for y in range(NY) for z in range(NZ)]
    return lax.ppermute(value, axis, perm)


def halves(value, dim):
    size = value.shape[dim] // 2
    return lax.slice_in_dim(value, 0, size, axis=dim), lax.slice_in_dim(value, size, 2 * size, axis=dim)


def gather_ring(own, dim, n, split):
    up, down = {0: own}, {0: own}
    for d in range(1, n // 2):
        up[d] = shift(up[d - 1], dim, -1)
        down[d] = shift(down[d - 1], dim, 1)
    first = shift(halves(up[n // 2 - 1], split)[0], dim, -1)
    second = shift(halves(down[n // 2 - 1], split)[1], dim, 1)
    near = [[up[d]] for d in range(n // 2)]
    far = [[down[d]] for d in range(n // 2 - 1, 0, -1)]
    return near + [[first, second]] + far


def add(a, b):
    return (a.astype(F32) + b.astype(F32)).astype(BF16)


def reduce_ring(parts, dim, n, split):
    first, second = halves(parts[n // 2], split)
    up = shift(first, dim, 1)
    down = shift(second, dim, -1)
    for d in range(n // 2 - 1, 0, -1):
        a, b = parts[d], parts[n - d]
        if d == n // 2 - 1:
            low, high = halves(a, split)
            a = jnp.concatenate([add(low, up), high], axis=split)
            low, high = halves(b, split)
            b = jnp.concatenate([low, add(high, down)], axis=split)
        else:
            a, b = add(a, up), add(b, down)
        up = shift(a, dim, 1)
        down = shift(b, dim, -1)
    return (parts[0].astype(F32) + up.astype(F32) + down.astype(F32)).astype(BF16)


def weight_grad_kernel(scale, nx, ny, idx_ref, gt_ref, ht_ref, *refs):
    x_refs, y_refs, out_ref = refs[:nx], refs[nx : nx + ny], refs[nx + ny]
    split = gt_ref.shape[0]
    xs = jnp.concatenate([r[...] for r in x_refs], axis=0)
    term = jnp.dot(gt_ref[...], xs, preferred_element_type=F32)
    out_ref[0, :split, :] = (term * scale).astype(out_ref.dtype)
    ys = jnp.concatenate([r[...] for r in y_refs], axis=0)
    term = jnp.dot(ht_ref[...], ys, preferred_element_type=F32)
    out_ref[0, split:, :] = (term * scale).astype(out_ref.dtype)


def weight_grads(idx, gt, ht, x_list, y_list, scale):
    count = idx.shape[0]
    columns = x_list[0].shape[1] * count // (NX * NC)
    piece = columns // count
    height = gt.shape[0] + ht.shape[0]
    rows = gt.shape[1]
    fixed = lambda a: pl.BlockSpec(a.shape, lambda j, idx: (0, 0))
    moving = lambda a: pl.BlockSpec((a.shape[0], piece), lambda j, idx: (0, idx[j]))
    return pl.pallas_call(
        lambda *refs: weight_grad_kernel(scale, len(x_list), len(y_list), *refs),
        grid_spec=pltpu.PrefetchScalarGridSpec(
            num_scalar_prefetch=1,
            grid=(count,),
            in_specs=[fixed(gt), fixed(ht)] + [moving(a) for a in x_list] + [moving(a) for a in y_list],
            out_specs=pl.BlockSpec((1, height, piece), lambda j, idx: (j, 0, 0)),
        ),
        out_shape=jax.ShapeDtypeStruct((count, height, piece), BF16),
        cost_estimate=pl.CostEstimate(
            flops=2 * rows * height * columns, bytes_accessed=2 * columns * (2 * rows + height), transcendentals=0
        ),
        name="weight_grads",
    )(idx, gt, ht, *x_list, *y_list)


def flat(groups):
    return [a for group in groups for a in group]


def swap_blocks(a, outer, inner, rows):
    return a.reshape(outer, inner, rows, a.shape[1]).swapaxes(0, 1).reshape(a.shape)


def body(layer_input, output_grad, gate_weight, up_weight, down_weight, block_lists, block_count):
    rows, d_model = layer_input.shape
    width = gate_weight.shape[1]
    blocks_here = width // BLOCK
    hid = lax.axis_index("hid")
    tok = lax.axis_index("tok")
    y, z = hid // NZ, hid % NZ
    x, c = tok // NC, tok % NC
    tok_rows = rows * NY * NZ
    weights = jnp.concatenate([gate_weight, up_weight], axis=1)

    local_blocks = hid * blocks_here + jnp.arange(blocks_here, dtype=jnp.int32)
    in_list = jnp.arange(block_lists.shape[1])[None, :] < block_count[:, None]
    hits = (block_lists[:, :, None] == local_blocks[None, None, :]) & in_list[:, :, None]
    active = jnp.any(hits, axis=1).astype(F32)
    owner_z = (z + jnp.arange(NZ)) % NZ
    owner_y = (y + jnp.arange(NY)) % NY
    owner = owner_y[None, :] * NZ + owner_z[:, None]
    tile = ((owner[:, :, None] * rows + jnp.arange(rows)[None, None, :]) // TILE).reshape(tok_rows, 1)
    row_active = jnp.zeros((tok_rows, blocks_here), F32)
    for t in range(block_count.shape[0]):
        row_active = jnp.where(tile == t, active[t][None, :], row_active)
    unit_mask = jnp.broadcast_to(row_active[:, :, None], (tok_rows, blocks_here, BLOCK)).reshape(tok_rows, width)

    near = gather_ring(layer_input, "y", NY, 1)
    near = jnp.concatenate([near[0][0], near[1][0], jnp.concatenate(near[2], axis=1), near[3][0]], axis=0)
    x_list = flat(gather_ring(near, "z", NZ, 0))
    near = gather_ring(output_grad, "z", NZ, 1)
    near = jnp.concatenate([g[0] if len(g) == 1 else jnp.concatenate(g, axis=1) for g in near], axis=0)
    y_list = flat(gather_ring(near, "y", NY, 0))

    pre = jnp.concatenate([jnp.dot(a, weights, preferred_element_type=F32) for a in x_list], axis=0)
    grad_hidden = jnp.concatenate(
        [lax.dot_general(a, down_weight, LAST, preferred_element_type=F32) for a in y_list], axis=0
    )
    grad_hidden = swap_blocks(grad_hidden, NY, NZ, rows)
    gate_pre, up_pre = pre[:, :width], pre[:, width:]
    sigmoid_g = jax.nn.sigmoid(gate_pre)
    silu_g = gate_pre * sigmoid_g
    hidden = (unit_mask * silu_g * up_pre).astype(BF16)
    grad_gate = (unit_mask * grad_hidden * up_pre * sigmoid_g * (1.0 + gate_pre * (1.0 - sigmoid_g))).astype(BF16)
    grad_up = (unit_mask * grad_hidden * silu_g).astype(BF16)
    grads = jnp.concatenate([grad_gate, grad_up], axis=1)

    cut = d_model // 2
    turned = swap_blocks(grads, NZ, NY, rows)
    per_z, per_y = rows * NY, rows * NZ

    def product(values, matrix):
        return lax.dot_general(values, matrix, LAST, preferred_element_type=F32).astype(BF16)

    far_z = product(grads[NZ // 2 * per_z : (NZ // 2 + 1) * per_z], weights[:cut])
    far_y = product(turned[NY // 2 * per_y : (NY // 2 + 1) * per_y], weights[cut:])
    scale = 1.0 / math.sqrt(tok_rows * NX * NC)
    owner_x = (x + jnp.arange(NX, dtype=jnp.int32)) % NX * NC
    gt, ht = grads.T, swap_blocks(hidden, NZ, NY, rows).T
    gt, ht, far_z, far_y = lax.optimization_barrier((gt, ht, far_z, far_y))
    terms = weight_grads(owner_x + (1 - c), gt, ht, x_list, y_list, scale)
    gt, ht, terms = lax.optimization_barrier((gt, ht, terms))
    mine = add(weight_grads(owner_x + c, gt, ht, x_list, y_list, scale), shift(terms, "c", 1))
    grads, turned, mine = lax.optimization_barrier((grads, turned, mine))

    part = product(grads, weights[:cut])
    parts = [part[r * per_z : (r + 1) * per_z] for r in range(NZ)]
    parts[NZ // 2] = far_z
    part = product(turned, weights[cut:])
    turned_parts = [part[r * per_y : (r + 1) * per_y] for r in range(NY)]
    turned_parts[NY // 2] = far_y
    part = reduce_ring(parts, "z", NZ, 0)
    left = reduce_ring([part[r * rows : (r + 1) * rows] for r in range(NY)], "y", NY, 1)
    part = reduce_ring(turned_parts, "y", NY, 0)
    right = reduce_ring([part[r * rows : (r + 1) * rows] for r in range(NZ)], "z", NZ, 1)
    input_grad = jnp.concatenate([left, right], axis=1)

    total = reduce_ring([mine[r] for r in range(NX)], "x", NX, 0)
    gate_grad = total[:width].T
    up_grad = total[width : 2 * width].T
    down_grad = total[2 * width :]
    return (input_grad, gate_grad, up_grad, down_grad)


def solution(mesh):
    in_specs = (
        P(("tok", "hid"), None),
        P(("tok", "hid"), None),
        P(None, "hid"),
        P(None, "hid"),
        P("hid", None),
        P("tok", None),
        P("tok"),
    )
    out_specs = (P(("tok", "hid"), None), P("tok", "hid"), P("tok", "hid"), P("hid", "tok"))
    return jax.shard_map(body, mesh=mesh, in_specs=in_specs, out_specs=out_specs, check_vma=False)
```

```python
import math

import jax
import jax.numpy as jnp
from jax import lax
from jax.experimental import pallas as pl
from jax.experimental.pallas import tpu as pltpu
from jax.sharding import PartitionSpec as P


BLOCK = 128
TILE = 128
NX, NC, NY, NZ = 4, 2, 4, 8
Y_ORDER, Z_ORDER = (0, 1, 3, 2), (0, 1, 7, 2, 6, 3, 5, 4)
LAST = (((1,), (1,)), ((), ()))
F32 = jnp.float32
BF16 = jnp.bfloat16


def shift(value, dim, step):
    if dim == "x":
        axis = "tok"
        perm = [(x * NC + c, (x + step) % NX * NC + c) for x in range(NX) for c in range(NC)]
    elif dim == "c":
        axis = "tok"
        perm = [(x * NC + c, x * NC + (c + step) % NC) for x in range(NX) for c in range(NC)]
    elif dim == "y":
        axis = "hid"
        perm = [(y * NZ + z, (y + step) % NY * NZ + z) for y in range(NY) for z in range(NZ)]
    else:
        axis = "hid"
        perm = [(y * NZ + z, y * NZ + (z + step) % NZ) for y in range(NY) for z in range(NZ)]
    return lax.ppermute(value, axis, perm)


def halves(value, dim):
    size = value.shape[dim] // 2
    return lax.slice_in_dim(value, 0, size, axis=dim), lax.slice_in_dim(value, size, 2 * size, axis=dim)


def gather_ring(own, dim, n, split):
    up, down = {0: own}, {0: own}
    for d in range(1, n // 2):
        up[d] = shift(up[d - 1], dim, -1)
        down[d] = shift(down[d - 1], dim, 1)
    first = shift(halves(up[n // 2 - 1], split)[0], dim, -1)
    second = shift(halves(down[n // 2 - 1], split)[1], dim, 1)
    near = [[up[d]] for d in range(n // 2)]
    far = [[down[d]] for d in range(n // 2 - 1, 0, -1)]
    return near + [[first, second]] + far


def add(*terms):
    total = terms[0].astype(F32)
    for term in terms[1:]:
        total = total + term.astype(F32)
    return total.astype(BF16)


def reduce_start(parts, dim, n, split):
    far = parts[n // 2]
    far = far[0] if len(far) == 1 else add(*far)
    first, second = halves(far, split)
    return shift(first, dim, 1), shift(second, dim, -1)


def reduce_next(parts, moved, n, split):
    up, down = moved
    a, b = parts[n // 2 - 1], parts[n // 2 + 1]
    lows, highs = zip(*[halves(t, split) for t in a])
    a = jnp.concatenate([add(*lows, up), add(*highs)], axis=split)
    lows, highs = zip(*[halves(t, split) for t in b])
    b = jnp.concatenate([add(*lows), add(*highs, down)], axis=split)
    return a, b


def reduce_step(parts, sums, dim, d, n):
    up, down = shift(sums[0], dim, 1), shift(sums[1], dim, -1)
    return add(*parts[d - 1], up), add(*parts[n - d + 1], down)


def reduce_direct(parts, dim, n):
    order = [d for k in range(n // 2, 0, -1) for d in ((k, -k) if k < n // 2 else (k,))]
    return add(*parts[0], *[shift(parts[d % n][0], dim, d) for d in order])


def pieces(value, size, order):
    found = {place: [value[k * size : (k + 1) * size]] for k, place in enumerate(order)}
    return [found[place] for place in range(len(order))]


def weight_grad_kernel(scale, nx, ny, idx_ref, gt_ref, ht_ref, *refs):
    x_refs, y_refs, out_ref = refs[:nx], refs[nx : nx + ny], refs[nx + ny]
    split = gt_ref.shape[0]
    xs = jnp.concatenate([r[...] for r in x_refs], axis=0)
    term = jnp.dot(gt_ref[...], xs, preferred_element_type=F32)
    out_ref[0, :split, :] = (term * scale).astype(out_ref.dtype)
    ys = jnp.concatenate([r[...] for r in y_refs], axis=0)
    term = jnp.dot(ht_ref[...], ys, preferred_element_type=F32)
    out_ref[0, split:, :] = (term * scale).astype(out_ref.dtype)


def weight_grads(idx, gt, ht, x_list, y_list, scale):
    count = idx.shape[0]
    columns = x_list[0].shape[1] * count // (NX * NC)
    piece = columns // count
    height = gt.shape[0] + ht.shape[0]
    rows = gt.shape[1]
    fixed = lambda a: pl.BlockSpec(a.shape, lambda j, idx: (0, 0))
    moving = lambda a: pl.BlockSpec((a.shape[0], piece), lambda j, idx: (0, idx[j]))
    return pl.pallas_call(
        lambda *refs: weight_grad_kernel(scale, len(x_list), len(y_list), *refs),
        grid_spec=pltpu.PrefetchScalarGridSpec(
            num_scalar_prefetch=1,
            grid=(count,),
            in_specs=[fixed(gt), fixed(ht)] + [moving(a) for a in x_list] + [moving(a) for a in y_list],
            out_specs=pl.BlockSpec((1, height, piece), lambda j, idx: (j, 0, 0)),
        ),
        out_shape=jax.ShapeDtypeStruct((count, height, piece), BF16),
        cost_estimate=pl.CostEstimate(
            flops=2 * rows * height * columns, bytes_accessed=2 * columns * (2 * rows + height), transcendentals=0
        ),
        name="weight_grads",
    )(idx, gt, ht, *x_list, *y_list)


def swap_blocks(a, outer, inner, rows):
    return a.reshape(outer, inner, rows, a.shape[1]).swapaxes(0, 1).reshape(a.shape)


def backward(layer_input, output_grad, gate_weight, up_weight, down_weight, block_lists, block_count):
    rows, d_model = layer_input.shape
    width = gate_weight.shape[1]
    blocks_here = width // BLOCK
    hid = lax.axis_index("hid")
    tok = lax.axis_index("tok")
    y, z = hid // NZ, hid % NZ
    x, c = tok // NC, tok % NC
    tok_rows = rows * NY * NZ
    local_blocks = hid * blocks_here + jnp.arange(blocks_here, dtype=jnp.int32)
    in_list = jnp.arange(block_lists.shape[1])[None, :] < block_count[:, None]
    hits = (block_lists[:, :, None] == local_blocks[None, None, :]) & in_list[:, :, None]
    active = jnp.any(hits, axis=1).astype(F32)
    owner_z = (z + jnp.array(Z_ORDER, jnp.int32)) % NZ
    owner_y = (y + jnp.array(Y_ORDER, jnp.int32)) % NY
    owner = owner_y[None, :] * NZ + owner_z[:, None]
    tile = ((owner[:, :, None] * rows + jnp.arange(rows)[None, None, :]) // TILE).reshape(tok_rows, 1)
    row_active = jnp.zeros((tok_rows, blocks_here), F32)
    for t in range(block_count.shape[0]):
        row_active = jnp.where(tile == t, active[t][None, :], row_active)
    unit_mask = jnp.broadcast_to(row_active[:, :, None], (tok_rows, blocks_here, BLOCK)).reshape(tok_rows, width)

    near = [g[0] if len(g) == 1 else jnp.concatenate(g, axis=1) for g in gather_ring(layer_input, "y", NY, 1)]
    x_near = jnp.concatenate([near[p] for p in Y_ORDER], axis=0)
    near = [g[0] if len(g) == 1 else jnp.concatenate(g, axis=1) for g in gather_ring(output_grad, "z", NZ, 1)]
    y_near = jnp.concatenate([near[p] for p in Z_ORDER], axis=0)
    x_near, y_near, gate_weight, up_weight = lax.optimization_barrier((x_near, y_near, gate_weight, up_weight))
    x_ring = gather_ring(x_near, "z", NZ, 0)
    y_ring = gather_ring(y_near, "y", NY, 0)
    weights = jnp.concatenate([gate_weight, up_weight], axis=1)
    x_list = [x_near] + [jnp.concatenate(x_ring[d] + x_ring[NZ - d], axis=0) for d in range(1, NZ // 2)]
    x_list.append(jnp.concatenate(x_ring[NZ // 2], axis=0))
    y_list = [y_near, jnp.concatenate(y_ring[1] + y_ring[3], axis=0), jnp.concatenate(y_ring[2], axis=0)]

    pre = [jnp.dot(a, weights, preferred_element_type=F32) for a in x_list]
    grad_hidden = jnp.concatenate(
        [lax.dot_general(a, down_weight, LAST, preferred_element_type=F32) for a in y_list], axis=0
    )
    grad_hidden = swap_blocks(grad_hidden, NY, NZ, rows)
    per_z, per_y = rows * NY, rows * NZ
    most = tok_rows - per_z

    def unit_grads(pre, grad_hidden, mask):
        gate_pre, up_pre = pre[:, :width], pre[:, width:]
        sigmoid_g = jax.nn.sigmoid(gate_pre)
        silu_g = gate_pre * sigmoid_g
        hidden = (mask * silu_g * up_pre).astype(BF16)
        grad_gate = (mask * grad_hidden * up_pre * sigmoid_g * (1.0 + gate_pre * (1.0 - sigmoid_g))).astype(BF16)
        grad_up = (mask * grad_hidden * silu_g).astype(BF16)
        return hidden, jnp.concatenate([grad_gate, grad_up], axis=1)

    def product(values, matrix):
        return lax.dot_general(values, matrix, LAST, preferred_element_type=F32).astype(BF16)

    cut = d_model // 2
    hidden_most, grads_most = unit_grads(jnp.concatenate(pre[:-1], axis=0), grad_hidden[:most], unit_mask[:most])
    part_most = product(grads_most, weights[:cut])
    hidden_last, grads_last = unit_grads(pre[-1], grad_hidden[most:], unit_mask[most:])
    part_last = product(grads_last, weights[:cut])
    z_parts = [None] * NZ
    for k, place in enumerate(Z_ORDER):
        z_parts[place] = [part_last if k == NZ - 1 else part_most[k * per_z : (k + 1) * per_z]]
    z_moved = reduce_start(z_parts, "z", NZ, 0)
    grads = jnp.concatenate([grads_most, grads_last], axis=0)
    turned = swap_blocks(grads, NZ, NY, rows)
    far = product(turned[tok_rows - per_y :], weights[cut:])
    y_moved = reduce_start([None, None, [far], None], "y", NY, 0)
    part = product(turned[: tok_rows - per_y], weights[cut:])
    y_parts = [None] * NY
    for k, place in enumerate(Y_ORDER):
        y_parts[place] = [far if k == NY - 1 else part[k * per_y : (k + 1) * per_y]]
    z_sums = reduce_next(z_parts, z_moved, NZ, 0)

    scale = 1.0 / math.sqrt(tok_rows * NX * NC)
    owner_x = (x + jnp.arange(NX, dtype=jnp.int32)) % NX * NC
    hidden = swap_blocks(jnp.concatenate([hidden_most, hidden_last], axis=0), NZ, NY, rows)
    gt, ht, _, _, _ = lax.optimization_barrier((grads.T, hidden.T, part, *z_sums))
    terms = weight_grads(owner_x + (1 - c), gt, ht, x_list, y_list, scale)
    *y_moved, terms = lax.optimization_barrier((*y_moved, terms))
    y_sums = reduce_next(y_parts, y_moved, NY, 0)
    other = shift(terms, "c", 1)
    z_sums = reduce_step(z_parts, z_sums, "z", NZ // 2 - 1, NZ)
    gt, ht, *_ = lax.optimization_barrier((gt, ht, *y_sums, *z_sums))
    mine = weight_grads(owner_x + c, gt, ht, x_list, y_list, scale)
    x_parts = [[mine[r], other[r]] for r in range(NX)]
    far = add(*x_parts[NX // 2])
    y_ends = shift(y_sums[0], "y", 1), shift(y_sums[1], "y", -1)
    *y_ends, far = lax.optimization_barrier((*y_ends, far))
    x_parts[NX // 2] = [far]
    x_moved = reduce_start(x_parts, "x", NX, 0)

    z_sums = reduce_step(z_parts, z_sums, "z", NZ // 2 - 2, NZ)
    z_ends = shift(z_sums[0], "z", 1), shift(z_sums[1], "z", -1)
    x_sums = reduce_next(x_parts, x_moved, NX, 0)
    *z_ends, a, b = lax.optimization_barrier((*z_ends, *x_sums))
    z_total = add(*z_parts[0], *z_ends)
    left = reduce_direct(pieces(z_total, rows, Y_ORDER), "y", NY)
    y_total = add(*y_parts[0], *y_ends)
    right = reduce_direct(pieces(y_total, rows, Z_ORDER), "z", NZ)
    input_grad = jnp.concatenate([left, right], axis=1)

    a = shift(a, "x", 1)
    b = shift(b, "x", -1)
    total = add(*x_parts[0], a, b)
    gate_grad = total[:width].T
    up_grad = total[width : 2 * width].T
    down_grad = total[2 * width :]
    return (input_grad, gate_grad, up_grad, down_grad)


def solution(mesh):
    in_specs = (
        P(("tok", "hid"), None),
        P(("tok", "hid"), None),
        P(None, "hid"),
        P(None, "hid"),
        P("hid", None),
        P("tok", None),
        P("tok"),
    )
    out_specs = (P(("tok", "hid"), None), P("tok", "hid"), P("tok", "hid"), P("hid", "tok"))
    return jax.shard_map(backward, mesh=mesh, in_specs=in_specs, out_specs=out_specs, check_vma=False)
```

```python
import math

import jax
import jax.numpy as jnp
from jax import lax
from jax.experimental import pallas as pl
from jax.experimental.pallas import tpu as pltpu
from jax.sharding import PartitionSpec as P


BLOCK = 128
TILE = 128
NX, NC, NY, NZ = 4, 2, 4, 8
Y_ORDER, Z_ORDER = (0, 1, 3, 2), (0, 1, 7, 2, 6, 3, 5, 4)
LAST = (((1,), (1,)), ((), ()))
F32 = jnp.float32
BF16 = jnp.bfloat16


def shift(value, dim, step):
    if dim == "x":
        axis = "tok"
        perm = [(x * NC + c, (x + step) % NX * NC + c) for x in range(NX) for c in range(NC)]
    elif dim == "c":
        axis = "tok"
        perm = [(x * NC + c, x * NC + (c + step) % NC) for x in range(NX) for c in range(NC)]
    elif dim == "y":
        axis = "hid"
        perm = [(y * NZ + z, (y + step) % NY * NZ + z) for y in range(NY) for z in range(NZ)]
    else:
        axis = "hid"
        perm = [(y * NZ + z, y * NZ + (z + step) % NZ) for y in range(NY) for z in range(NZ)]
    return lax.ppermute(value, axis, perm)


def halves(value, dim):
    size = value.shape[dim] // 2
    return lax.slice_in_dim(value, 0, size, axis=dim), lax.slice_in_dim(value, size, 2 * size, axis=dim)


def gather_ring(own, dim, n, split):
    up, down = {0: own}, {0: own}
    for d in range(1, n // 2):
        up[d] = shift(up[d - 1], dim, -1)
        down[d] = shift(down[d - 1], dim, 1)
    first = shift(halves(up[n // 2 - 1], split)[0], dim, -1)
    second = shift(halves(down[n // 2 - 1], split)[1], dim, 1)
    near = [[up[d]] for d in range(n // 2)]
    far = [[down[d]] for d in range(n // 2 - 1, 0, -1)]
    return near + [[first, second]] + far


def add(*terms):
    total = terms[0].astype(F32)
    for term in terms[1:]:
        total = total + term.astype(F32)
    return total.astype(BF16)


def reduce_start(parts, dim, n, split):
    far = parts[n // 2]
    far = far[0] if len(far) == 1 else add(*far)
    first, second = halves(far, split)
    return shift(first, dim, 1), shift(second, dim, -1)


def reduce_next(parts, moved, n, split):
    up, down = moved
    a, b = parts[n // 2 - 1], parts[n // 2 + 1]
    lows, highs = zip(*[halves(t, split) for t in a])
    a = jnp.concatenate([add(*lows, up), add(*highs)], axis=split)
    lows, highs = zip(*[halves(t, split) for t in b])
    b = jnp.concatenate([add(*lows), add(*highs, down)], axis=split)
    return a, b


def reduce_direct(parts, dim, n):
    order = [d for k in range(n // 2, 0, -1) for d in ((k, -k) if k < n // 2 else (k,))]
    return add(*parts[0], *[shift(parts[d % n][0], dim, d) for d in order])


def pieces(value, size, order):
    found = {place: [value[k * size : (k + 1) * size]] for k, place in enumerate(order)}
    return [found[place] for place in range(len(order))]


def weight_grad_kernel(scale, nx, ny, idx_ref, gt_ref, ht_ref, *refs):
    x_refs, y_refs, out_ref = refs[:nx], refs[nx : nx + ny], refs[nx + ny]
    split = gt_ref.shape[0]
    xs = jnp.concatenate([r[...] for r in x_refs], axis=0)
    term = jnp.dot(gt_ref[...], xs, preferred_element_type=F32)
    out_ref[0, :split, :] = (term * scale).astype(out_ref.dtype)
    ys = jnp.concatenate([r[...] for r in y_refs], axis=0)
    term = jnp.dot(ht_ref[...], ys, preferred_element_type=F32)
    out_ref[0, split:, :] = (term * scale).astype(out_ref.dtype)


def weight_grads(idx, gt, ht, x_list, y_list, scale):
    count = idx.shape[0]
    columns = x_list[0].shape[1] * count // (NX * NC)
    piece = columns // count
    height = gt.shape[0] + ht.shape[0]
    rows = gt.shape[1]
    fixed = lambda a: pl.BlockSpec(a.shape, lambda j, idx: (0, 0))
    moving = lambda a: pl.BlockSpec((a.shape[0], piece), lambda j, idx: (0, idx[j]))
    return pl.pallas_call(
        lambda *refs: weight_grad_kernel(scale, len(x_list), len(y_list), *refs),
        grid_spec=pltpu.PrefetchScalarGridSpec(
            num_scalar_prefetch=1,
            grid=(count,),
            in_specs=[fixed(gt), fixed(ht)] + [moving(a) for a in x_list] + [moving(a) for a in y_list],
            out_specs=pl.BlockSpec((1, height, piece), lambda j, idx: (j, 0, 0)),
        ),
        out_shape=jax.ShapeDtypeStruct((count, height, piece), BF16),
        cost_estimate=pl.CostEstimate(
            flops=2 * rows * height * columns, bytes_accessed=2 * columns * (2 * rows + height), transcendentals=0
        ),
        name="weight_grads",
    )(idx, gt, ht, *x_list, *y_list)


def swap_blocks(a, outer, inner, rows):
    return a.reshape(outer, inner, rows, a.shape[1]).swapaxes(0, 1).reshape(a.shape)


def backward(layer_input, output_grad, gate_weight, up_weight, down_weight, block_lists, block_count):
    rows, d_model = layer_input.shape
    width = gate_weight.shape[1]
    blocks_here = width // BLOCK
    hid = lax.axis_index("hid")
    tok = lax.axis_index("tok")
    y, z = hid // NZ, hid % NZ
    x, c = tok // NC, tok % NC
    tok_rows = rows * NY * NZ
    local_blocks = hid * blocks_here + jnp.arange(blocks_here, dtype=jnp.int32)
    in_list = jnp.arange(block_lists.shape[1])[None, :] < block_count[:, None]
    hits = (block_lists[:, :, None] == local_blocks[None, None, :]) & in_list[:, :, None]
    active = jnp.any(hits, axis=1).astype(F32)
    owner_z = (z + jnp.array(Z_ORDER, jnp.int32)) % NZ
    owner_y = (y + jnp.array(Y_ORDER, jnp.int32)) % NY
    owner = owner_y[None, :] * NZ + owner_z[:, None]
    tile = ((owner[:, :, None] * rows + jnp.arange(rows)[None, None, :]) // TILE).reshape(tok_rows, 1)
    row_active = jnp.zeros((tok_rows, blocks_here), F32)
    for t in range(block_count.shape[0]):
        row_active = jnp.where(tile == t, active[t][None, :], row_active)
    unit_mask = jnp.broadcast_to(row_active[:, :, None], (tok_rows, blocks_here, BLOCK)).reshape(tok_rows, width)

    near = [g[0] if len(g) == 1 else jnp.concatenate(g, axis=1) for g in gather_ring(layer_input, "y", NY, 1)]
    x_near = jnp.concatenate([near[p] for p in Y_ORDER], axis=0)
    near = [g[0] if len(g) == 1 else jnp.concatenate(g, axis=1) for g in gather_ring(output_grad, "z", NZ, 1)]
    y_near = jnp.concatenate([near[p] for p in Z_ORDER], axis=0)
    x_near, y_near, gate_weight, up_weight = lax.optimization_barrier((x_near, y_near, gate_weight, up_weight))
    x_ring = gather_ring(x_near, "z", NZ, 0)
    y_ring = gather_ring(y_near, "y", NY, 0)
    weights = jnp.concatenate([gate_weight, up_weight], axis=1)
    x_list = [x_near] + [jnp.concatenate(x_ring[d] + x_ring[NZ - d], axis=0) for d in range(1, NZ // 2)]
    x_list.append(jnp.concatenate(x_ring[NZ // 2], axis=0))
    y_list = [y_near, jnp.concatenate(y_ring[1] + y_ring[3], axis=0), jnp.concatenate(y_ring[2], axis=0)]

    pre = [jnp.dot(a, weights, preferred_element_type=F32) for a in x_list]
    grad_hidden = jnp.concatenate(
        [lax.dot_general(a, down_weight, LAST, preferred_element_type=F32) for a in y_list], axis=0
    )
    grad_hidden = swap_blocks(grad_hidden, NY, NZ, rows)
    per_z, per_y = rows * NY, rows * NZ
    most = tok_rows - per_z

    def unit_grads(pre, grad_hidden, mask):
        gate_pre, up_pre = pre[:, :width], pre[:, width:]
        sigmoid_g = jax.nn.sigmoid(gate_pre)
        silu_g = gate_pre * sigmoid_g
        hidden = (mask * silu_g * up_pre).astype(BF16)
        grad_gate = (mask * grad_hidden * up_pre * sigmoid_g * (1.0 + gate_pre * (1.0 - sigmoid_g))).astype(BF16)
        grad_up = (mask * grad_hidden * silu_g).astype(BF16)
        return hidden, jnp.concatenate([grad_gate, grad_up], axis=1)

    def product(values, matrix):
        return lax.dot_general(values, matrix, LAST, preferred_element_type=F32).astype(BF16)

    cut = d_model // 2
    hidden_most, grads_most = unit_grads(jnp.concatenate(pre[:-1], axis=0), grad_hidden[:most], unit_mask[:most])
    part_most = product(grads_most, weights[:cut])
    hidden_last, grads_last = unit_grads(pre[-1], grad_hidden[most:], unit_mask[most:])
    part_last = product(grads_last, weights[:cut])
    z_parts = [None] * NZ
    for k, place in enumerate(Z_ORDER):
        z_parts[place] = [part_last if k == NZ - 1 else part_most[k * per_z : (k + 1) * per_z]]
    z_moved = reduce_start(z_parts, "z", NZ, 0)
    grads = jnp.concatenate([grads_most, grads_last], axis=0)
    turned = swap_blocks(grads, NZ, NY, rows)
    far = product(turned[tok_rows - per_y :], weights[cut:])
    y_moved = reduce_start([None, None, [far], None], "y", NY, 0)
    part = product(turned[: tok_rows - per_y], weights[cut:])
    y_parts = [None] * NY
    for k, place in enumerate(Y_ORDER):
        y_parts[place] = [far if k == NY - 1 else part[k * per_y : (k + 1) * per_y]]
    z_sums = lax.optimization_barrier(reduce_next(z_parts, z_moved, NZ, 0))

    z_moved = shift(z_sums[0], "z", 1), shift(z_sums[1], "z", -1)
    scale = 1.0 / math.sqrt(tok_rows * NX * NC)
    owner_x = (x + jnp.arange(NX, dtype=jnp.int32)) % NX * NC
    hidden = swap_blocks(jnp.concatenate([hidden_most, hidden_last], axis=0), NZ, NY, rows)
    gt, ht, _, _, _ = lax.optimization_barrier((grads.T, hidden.T, part, *z_sums))
    terms = weight_grads(owner_x + (1 - c), gt, ht, x_list, y_list, scale)
    *y_moved, terms = lax.optimization_barrier((*y_moved, terms))
    y_sums = lax.optimization_barrier(reduce_next(y_parts, y_moved, NY, 0))
    y_ends = shift(y_sums[0], "y", 1), shift(y_sums[1], "y", -1)
    other = shift(terms, "c", 1)
    gt, ht, *_ = lax.optimization_barrier((gt, ht, *y_sums))
    mine = weight_grads(owner_x + c, gt, ht, x_list, y_list, scale)
    x_parts = [[mine[r], other[r]] for r in range(NX)]
    far = add(*x_parts[NX // 2])
    *z_moved, far = lax.optimization_barrier((*z_moved, far))
    x_parts[NX // 2] = [far]
    x_moved = reduce_start(x_parts, "x", NX, 0)

    d = NZ // 2 - 2
    z_sums = lax.optimization_barrier((add(*z_parts[d], z_moved[0]), add(*z_parts[NZ - d], z_moved[1])))
    z_moved = shift(z_sums[0], "z", 1), shift(z_sums[1], "z", -1)
    z_sums = lax.optimization_barrier((add(*z_parts[d - 1], z_moved[0]), add(*z_parts[NZ - d + 1], z_moved[1])))
    z_ends = shift(z_sums[0], "z", 1), shift(z_sums[1], "z", -1)
    x_sums = reduce_next(x_parts, x_moved, NX, 0)
    *y_ends, a, b = lax.optimization_barrier((*y_ends, *x_sums))
    z_total = add(*z_parts[0], *z_ends)
    left = reduce_direct(pieces(z_total, rows, Y_ORDER), "y", NY)
    y_total = add(*y_parts[0], *y_ends)
    right = reduce_direct(pieces(y_total, rows, Z_ORDER), "z", NZ)
    input_grad = jnp.concatenate([left, right], axis=1)

    a = shift(a, "x", 1)
    b = shift(b, "x", -1)
    total = add(*x_parts[0], a, b)
    gate_grad = total[:width].T
    up_grad = total[width : 2 * width].T
    down_grad = total[2 * width :]
    return (input_grad, gate_grad, up_grad, down_grad)


def solution(mesh):
    in_specs = (
        P(("tok", "hid"), None),
        P(("tok", "hid"), None),
        P(None, "hid"),
        P(None, "hid"),
        P("hid", None),
        P("tok", None),
        P("tok"),
    )
    out_specs = (P(("tok", "hid"), None), P("tok", "hid"), P("tok", "hid"), P("hid", "tok"))
    return jax.shard_map(backward, mesh=mesh, in_specs=in_specs, out_specs=out_specs, check_vma=False)
```
